32 devices in a mesh: ct: 16 (over z, y, core), bl: 2 (over x).
Axes of the slice: x: 2, y: 2, z: 4, core: 2. Of those that a mesh axis runs over, the one named last changes fastest.
Arguments:
- samples: bfloat16 [512, 65536], P('ct', 'bl'), may hold values from -6 to 6
- history: bfloat16 [512, 1536], P('ct'), may hold values from -6 to 6
- tile_cell: int32 [256, 10], P('ct'), may hold values from 0 to 3
- tile_weight: float32 [256, 10], P('ct'), may hold values from 0.25 to 4
Outputs:
- grid: float32 [4, 256, 2, 128, 128], P('bl', 'ct')
The draws below stay inside these ranges and needn't reach their ends.
All inputs are finite; a program needn't handle non-finite values.
Results may differ from the reference program's by a relative error of at most 0.0048.
Values may be sent and summed in bfloat16 or wider, within the bound.
No kernel may reach another device: no remote copies, remote signals or barrier semaphores. Data moves between devices by JAX's collectives and lax.ppermute only.
A program may use at most 128 MiB of HBM per device.

```python
import math
import jax
import jax.numpy as jnp
import numpy as np
from jax import lax

CH = 256
BLOCK = 128
TAPS = 4
SPECTRA = 128
FRAME = 512
INPUTS = 512
NTILE = 10
NCELL = 4


def touch_ends(values, own_key, low, largest):
    spot = [jax.random.randint(jax.random.fold_in(own_key, axis), (), 0, length) for axis, length in enumerate(values.shape)]
    main_axis = values.shape.index(max(values.shape))
    next_to = spot[:main_axis] + [(spot[main_axis] + 1) % values.shape[main_axis]] + spot[main_axis + 1:]
    return values.at[tuple(spot)].set(low).at[tuple(next_to)].set(largest)


def shard_levels(key, shape, cuts, least, high):
    loudness, own = 1.0, jax.random.fold_in(key, 6)
    for dim, parts in cuts:
        heights = jnp.exp(jax.random.uniform(jax.random.fold_in(own, dim), (parts,), jnp.float32, least / len(cuts), high / len(cuts)))
        loudness = loudness * jnp.repeat(heights, shape[dim] // parts).reshape([-1 if axis == dim else 1 for axis in range(len(shape))])
    return loudness


def rank_bounds(amount, slope):
    weights = [(1 << 20) // math.isqrt(grade ** slope) + 1 for grade in range(1, amount + 1)]
    scale = 1 + sum(weights) // (1 << 30)
    return np.cumsum(np.array([max(1, weight // scale) for weight in weights]))


def ranked_ids(stream_key, shape, count, skew):
    listing = rank_bounds(count, skew)
    lot = jax.random.randint(jax.random.fold_in(stream_key, 1), shape, 0, int(listing[count - 1]))
    standing = jnp.searchsorted(jnp.asarray(listing, jnp.int32), lot, side="right")
    return jax.random.permutation(jax.random.fold_in(stream_key, 2), count)[standing].astype(jnp.int32)


def scatter_about(stream_key, shape, scale, limit, pieces=(), kind=jnp.bfloat16):
    result = scale * jax.random.normal(stream_key, shape, jnp.float32)
    if pieces:
        result = result * shard_levels(stream_key, shape, pieces, -0.22, 0.18)
    return jnp.clip(result, -limit, limit).astype(kind)


def setup_inputs(seed: int = 0) -> dict:
    streams_of = jax.random.split(jax.random.key(seed), 5)
    samples = scatter_about(streams_of[0], (INPUTS, SPECTRA * FRAME), 1.0, 6.0, ((0, 16), (1, 2)))
    history = scatter_about(streams_of[1], (INPUTS, (TAPS - 1) * FRAME), 1.0, 6.0, ((0, 16),))
    tile_cell = touch_ends(ranked_ids(streams_of[2], (CH, NTILE), NCELL, 2), jax.random.fold_in(streams_of[2], 3), 0, NCELL - 1).astype(jnp.int32)
    tile_weight = jnp.clip(jnp.exp(math.log(4.0) - 2.7725887 * jax.random.uniform(streams_of[3], (CH, NTILE), jnp.float32) ** shard_levels(streams_of[3], (CH, NTILE), ((0, 16),), -0.2, 0.2)), 0.25, 4.0)
    return dict(samples=samples, history=history, tile_cell=tile_cell, tile_weight=tile_weight)


def filter_table():
    span = TAPS * FRAME
    sample_pos = jnp.arange(span, dtype=jnp.float32) + 0.5
    window = jnp.sinc(sample_pos / FRAME - TAPS / 2.0) * (0.5 - 0.5 * jnp.cos(2.0 * math.pi * sample_pos / span))
    phase_int = jnp.arange(FRAME, dtype=jnp.int32)[:, None] * jnp.arange(CH, dtype=jnp.int32)[None, :] % FRAME
    angle = phase_int.astype(jnp.float32) * (2.0 * math.pi / FRAME)
    basis = jnp.concatenate([jnp.cos(angle), -jnp.sin(angle)], axis=1)
    table = window.reshape(TAPS, FRAME)[:, :, None] * basis[None] * (2.0 / math.sqrt(FRAME))
    return table.astype(jnp.bfloat16)

def reference(samples, history, tile_cell, tile_weight):
    blocks = INPUTS // BLOCK
    table = filter_table().astype(jnp.float32)
    whole = jnp.concatenate([history, samples], axis=1).reshape(blocks, BLOCK, SPECTRA + TAPS - 1, FRAME)

    def one_block(group):
        group_wide = group.astype(jnp.float32)
        accum = jnp.zeros((2 * CH, BLOCK, SPECTRA), jnp.float32)
        for tap_index in range(TAPS):
            accum = accum + jnp.einsum('psn,nk->kps', group_wide[:, tap_index:tap_index + SPECTRA], table[tap_index], precision=lax.Precision.HIGHEST)
        return accum.astype(jnp.bfloat16)
    spectra = lax.map(one_block, whole)
    spectra = spectra.reshape(blocks, 2, CH, BLOCK, SPECTRA).transpose(2, 1, 0, 3, 4).reshape(CH, 2, INPUTS, SPECTRA)
    row_list = []
    col_list = []
    for row_block in range(blocks):
        for col_block in range(row_block, blocks):
            row_list.append(row_block)
            col_list.append(col_block)
    rows_np = np.array(row_list, dtype=np.int32)
    cols_np = np.array(col_list, dtype=np.int32)
    cell_ids = jnp.arange(NCELL, dtype=jnp.int32)
    norm_scale = 1.0 / math.sqrt(SPECTRA)

    def one_channel(items):
        chan, cells_row, weight_row = items
        data = chan.astype(jnp.float32)
        products = jnp.einsum('aps,bqs->abpq', data, data, precision=lax.Precision.HIGHEST)
        real_part = products[0, 0] + products[1, 1]
        imag_part = products[1, 0] - products[0, 1]
        visibility = jnp.stack([real_part, imag_part]).reshape(2, blocks, BLOCK, blocks, BLOCK)
        tiles = visibility[:, rows_np, :, cols_np, :]
        selector = (cells_row[None, :] == cell_ids[:, None]).astype(jnp.float32) * (weight_row * norm_scale)[None, :]
        return jnp.einsum('et,txpq->expq', selector, tiles, precision=lax.Precision.HIGHEST)
    grid = lax.map(one_channel, (spectra, tile_cell, tile_weight))
    return grid.transpose(1, 0, 2, 3, 4)
```

```python
import math

import jax
import jax.numpy as jnp
import numpy as np
from jax import lax
from jax.experimental import pallas as pl
from jax.experimental.pallas import tpu as pltpu
from jax.sharding import PartitionSpec as P

CH = 256
BLOCK = 128
TAPS = 4
SPECTRA = 128
CELL_DEV = 2
FRAME = 512
LANES = 128
SUBLANES = 8
HALO = TAPS - 1
STEP = 8


def table_rows():
    span = TAPS * FRAME
    sample_pos = np.arange(span, dtype=np.float64) + 0.5
    window = np.sinc(sample_pos / FRAME - TAPS / 2.0) * (
        0.5 - 0.5 * np.cos(2.0 * math.pi * sample_pos / span)
    )
    phase = np.arange(CH, dtype=np.int64)[:, None] * np.arange(FRAME, dtype=np.int64)[None, :] % FRAME
    angle = phase * (2.0 * math.pi / FRAME)
    basis = np.concatenate([np.cos(angle), -np.sin(angle)], axis=0)
    table = basis[:, None, :] * window.reshape(1, TAPS, FRAME) * (2.0 / math.sqrt(FRAME))
    return table.reshape(2 * CH, span).astype(np.float32).astype(jnp.bfloat16)


def chunk_table(groups, first, count):
    rows = table_rows().reshape(2, groups, CH // groups, TAPS * FRAME)
    rows = rows[:, :, first : first + count].transpose(1, 2, 0, 3)
    return np.ascontiguousarray(rows).reshape(2 * groups * count, TAPS * FRAME)


def channelize(samples, table, halo, so_far, first, steps, groups):
    inputs, length = samples.shape
    total = length // FRAME // STEP
    parts = STEP * inputs // LANES
    rows = table.shape[0] // groups * parts

    def body(*refs):
        refs = list(refs)
        index = refs.pop(0)
        now, prior, tab = refs[:3]
        out = refs[-1]
        before = prior[:, (STEP - HALO) * FRAME :]
        if halo is not None:
            received = jnp.where(index[0] == 0, refs[3][...], refs[4][...])
            before = received if steps == 1 else jnp.where(pl.program_id(0) == 0, received, before)
        extended = jnp.concatenate([before, now[...]], axis=1)
        window = jnp.concatenate(
            [extended[:, s * FRAME : (s + TAPS) * FRAME] for s in range(STEP)], axis=0
        )
        accum = lax.dot_general(
            tab[...], window, (((1,), (1,)), ((), ())), preferred_element_type=jnp.float32
        )
        pieces = [
            accum[:, part * LANES : (part + 1) * LANES].reshape(groups, -1, LANES)
            for part in range(parts)
        ]
        out[...] = jnp.concatenate(pieces, axis=1).astype(jnp.bfloat16)

    whole = lambda shape: pl.BlockSpec(shape, lambda i, *_: (0,) * len(shape))
    in_specs = [
        pl.BlockSpec((inputs, STEP * FRAME), lambda i, *_: (0, first + i)),
        pl.BlockSpec((inputs, STEP * FRAME), lambda i, *_: (0, jnp.maximum(first + i - 1, 0))),
        whole(table.shape),
    ]
    args = [samples, samples, table]
    index = jnp.zeros((1,), jnp.int32)
    if halo is not None:
        index = halo[0]
        in_specs += [whole(halo[1].shape), whole(halo[2].shape)]
        args += halo[1:]
    aliases = {}
    if so_far is not None:
        aliases = {len(args) + 1: 0}
        in_specs.append(pl.BlockSpec(memory_space=pl.ANY))
        args.append(so_far)
    return pl.pallas_call(
        body,
        grid_spec=pltpu.PrefetchScalarGridSpec(
            num_scalar_prefetch=1,
            grid=(steps,),
            in_specs=in_specs,
            out_specs=pl.BlockSpec((groups, rows, LANES), lambda i, *_: (0, first + i, 0)),
        ),
        out_shape=jax.ShapeDtypeStruct((groups, total * rows, LANES), jnp.bfloat16),
        input_output_aliases=aliases,
        name="channelize",
    )(index, *args)


def lane_exchange(tiles, width):
    count = len(tiles)
    lane = lax.broadcasted_iota(jnp.int32, tiles[0].shape, 1)
    size = count // 2
    while size:
        span = size * width
        upper = (lane // span) % 2 == 1
        done = list(tiles)
        for a in range(count):
            if a & size:
                continue
            low, high = tiles[a], tiles[a | size]
            done[a] = jnp.where(upper, pltpu.roll(high, span, 1), low)
            done[a | size] = jnp.where(upper, high, pltpu.roll(low, LANES - span, 1))
        tiles = done
        size //= 2
    return tiles


def correlate(turned, index, tile_cell, tile_weight, grid_so_far, first, channels, inputs_dev):
    ct_size, bl_size, rows, _ = turned.shape
    near = BLOCK // inputs_dev
    blocks = ct_size // near
    cells = CELL_DEV * bl_size
    own_channels = tile_cell.shape[0]
    group = own_channels // bl_size
    fresh = grid_so_far is None
    pitch = SPECTRA + 1
    per_bl = rows // SUBLANES

    def body(index_ref, cell_ref, weight_ref, src, *rest):
        if fresh:
            out, away, sums, columns = rest
        else:
            _, out, away, sums, columns = rest
        mine = index_ref[0]
        local = pl.program_id(0)
        channel = mine * group + first + local

        @pl.when(local == 0)
        def _():
            def relay(step, carry):
                top = pl.multiple_of(step * 2 * SUBLANES, 2 * SUBLANES)
                for b in range(bl_size):
                    for block in range(blocks):
                        loaded = [
                            src[block * near + a, b, pl.ds(top, 2 * SUBLANES), :].astype(jnp.float32)
                            for a in range(near)
                        ]
                        for half in range(2):
                            tiles = [t[half * SUBLANES : (half + 1) * SUBLANES] for t in loaded]
                            for s, tile in enumerate(lane_exchange(tiles, inputs_dev)):
                                row = b * per_bl * near + (step * 2 + half) * near + s
                                columns[block, pl.ds(row, SUBLANES, stride=pitch), :] = tile
                return carry

            lax.fori_loop(0, rows // (2 * SUBLANES), relay, 0)

        right = []
        left = []
        for block in range(blocks):
            parts = [
                columns[block, pl.ds((2 * local + part) * pitch, SPECTRA), :] for part in range(2)
            ]
            right.append(jnp.concatenate(parts, axis=0).astype(jnp.bfloat16))
            real, imag = [p.T.astype(jnp.bfloat16) for p in parts]
            left.append(
                jnp.concatenate(
                    [
                        jnp.concatenate([real, imag], axis=1),
                        jnp.concatenate([imag, -real], axis=1),
                    ],
                    axis=0,
                )
            )
        sums[...] = jnp.zeros_like(sums)
        tile = 0
        for row in range(blocks):
            for col in range(row, blocks):
                product = jnp.dot(left[row], right[col], preferred_element_type=jnp.float32)
                cell = cell_ref[channel, tile]
                weight = weight_ref[channel, tile] * (1.0 / math.sqrt(SPECTRA))
                sums[cell] += product * weight
                tile += 1
        for e in range(CELL_DEV):
            out[e, 0] = sums[mine * CELL_DEV + e].reshape(2, BLOCK, BLOCK)
        for step in range(1, bl_size):
            to = lax.rem(mine + step, bl_size)
            for e in range(CELL_DEV):
                away[step - 1, 0, e] = (
                    sums[to * CELL_DEV + e].reshape(2, BLOCK, BLOCK).astype(jnp.bfloat16)
                )

    in_specs = [pl.BlockSpec(turned.shape, lambda i, *_: (0, 0, 0, 0))]
    if not fresh:
        in_specs.append(pl.BlockSpec(memory_space=pl.ANY))
    return pl.pallas_call(
        body,
        grid_spec=pltpu.PrefetchScalarGridSpec(
            num_scalar_prefetch=3,
            grid=(channels,),
            in_specs=in_specs,
            out_specs=(
                pl.BlockSpec(
                    (CELL_DEV, 1, 2, BLOCK, BLOCK),
                    lambda i, index_ref, *_: (0, index_ref[0] * group + first + i, 0, 0, 0),
                ),
                pl.BlockSpec(
                    (bl_size - 1, 1, CELL_DEV, 2, BLOCK, BLOCK), lambda i, *_: (0, i, 0, 0, 0, 0)
                ),
            ),
            scratch_shapes=[
                pltpu.VMEM((cells, 2 * BLOCK, BLOCK), jnp.float32),
                pltpu.VMEM((blocks, SUBLANES * pitch, LANES), jnp.float32),
            ],
        ),
        out_shape=(
            jax.ShapeDtypeStruct((CELL_DEV, own_channels, 2, BLOCK, BLOCK), jnp.float32),
            jax.ShapeDtypeStruct(
                (bl_size - 1, channels, CELL_DEV, 2, BLOCK, BLOCK), jnp.bfloat16
            ),
        ),
        input_output_aliases={} if fresh else {4: 0},
        name="correlate",
    )(index, tile_cell, tile_weight, turned, *(() if fresh else (grid_so_far,)))


def fill_in(grid_so_far, received, index, first, bl_size):
    steps, channels = received.shape[:2]
    group = grid_so_far.shape[1] // bl_size

    def body(index_ref, src, _, out):
        for e in range(CELL_DEV):
            out[e] = src[0, :, e].astype(jnp.float32)

    def place(d, index_ref):
        origin = lax.rem(index_ref[0] + bl_size - 1 - d, bl_size)
        return (0, (origin * group + first) // channels, 0, 0, 0)

    return pl.pallas_call(
        body,
        grid_spec=pltpu.PrefetchScalarGridSpec(
            num_scalar_prefetch=1,
            grid=(steps,),
            in_specs=[
                pl.BlockSpec(
                    (1, channels, CELL_DEV, 2, BLOCK, BLOCK), lambda d, *_: (d, 0, 0, 0, 0, 0)
                ),
                pl.BlockSpec(memory_space=pl.ANY),
            ],
            out_specs=pl.BlockSpec((CELL_DEV, channels, 2, BLOCK, BLOCK), place),
        ),
        out_shape=jax.ShapeDtypeStruct(grid_so_far.shape, grid_so_far.dtype),
        input_output_aliases={2: 0},
        name="fill_in",
    )(index, received, grid_so_far)


def fast_shards(samples, history, tile_cell, tile_weight):
    ct_size = lax.axis_size("ct")
    bl_size = lax.axis_size("bl")
    index = lax.axis_index("bl").reshape(1).astype(jnp.int32)
    inputs_dev = samples.shape[0]
    spec_dev = samples.shape[1] // FRAME
    groups = ct_size * bl_size
    steps = spec_dev // STEP
    count = SUBLANES // 2
    chunks = range(0, CH // groups, count)

    behind = from_behind(samples[:, (spec_dev - HALO) * FRAME :], "bl", 1)
    halo = (index, history, behind)
    received = []
    for number, first in enumerate(chunks):
        table = jnp.asarray(chunk_table(groups, first, count))
        if number == 0:
            spectra = channelize(samples, table, None, None, 1, steps - 1, groups)
            spectra = channelize(samples, table, halo, spectra, 0, 1, groups)
        else:
            spectra = channelize(samples, table, halo, None, 0, steps, groups)
        turned = lax.all_to_all(spectra, ("ct", "bl"), 0, 0, tiled=True)
        received.append(turned.reshape(ct_size, bl_size, -1, LANES))
    grid = None
    swapped = []
    for first, turned in zip(chunks, received):
        grid, away = correlate(turned, index, tile_cell, tile_weight, grid, first, count, inputs_dev)
        back = []
        for step in range(1, bl_size):
            pairs = [(i, (i + step) % bl_size) for i in range(bl_size)]
            back.append(lax.ppermute(away[step - 1], "bl", pairs))
        swapped.append(jnp.stack(back))
    for first, back in zip(chunks, swapped):
        grid = fill_in(grid, back, index, first, bl_size)
    return grid


def fits(mesh, samples):
    ct_size, bl_size = mesh.shape["ct"], mesh.shape["bl"]
    inputs = samples.shape[0]
    spec_dev = samples.shape[1] // FRAME // bl_size
    inputs_dev = inputs // ct_size
    groups = ct_size * bl_size
    return (
        bl_size > 1
        and inputs_dev % 16 == 0
        and LANES % inputs_dev == 0
        and STEP * inputs_dev % LANES == 0
        and spec_dev % STEP == 0
        and spec_dev > STEP
        and inputs % BLOCK == 0
        and CH % groups == 0
        and CH // groups % (SUBLANES // 2) == 0
    )


def from_behind(value, axis, by):
    size = lax.axis_size(axis)
    pairs = [(i, i + by) for i in range(size) if 0 <= i + by < size]
    return lax.ppermute(value, axis, pairs)


def filter_table():
    span = TAPS * FRAME
    sample_pos = jnp.arange(span, dtype=jnp.float32) + 0.5
    window = jnp.sinc(sample_pos / FRAME - TAPS / 2.0) * (
        0.5 - 0.5 * jnp.cos(2.0 * math.pi * sample_pos / span)
    )
    phase_int = (
        jnp.arange(FRAME, dtype=jnp.int32)[:, None]
        * jnp.arange(CH, dtype=jnp.int32)[None, :]
        % FRAME
    )
    angle = phase_int.astype(jnp.float32) * (2.0 * math.pi / FRAME)
    basis = jnp.concatenate([jnp.cos(angle), -jnp.sin(angle)], axis=1)
    table = window.reshape(TAPS, FRAME)[:, :, None] * basis[None] * (2.0 / math.sqrt(FRAME))
    return table.astype(jnp.bfloat16)


def cell_selector(tile_cell, weights, tri_index, is_valid, cell_count):
    picked = jnp.take(tile_cell, tri_index, axis=1)
    picked_weight = jnp.take(weights, tri_index, axis=1) * is_valid
    cell_ids = lax.broadcasted_iota(jnp.int32, (cell_count, 1, 1), 0)
    return (picked[None] == cell_ids).astype(jnp.float32) * picked_weight[None]


def general_shards(samples, history, tile_cell, tile_weight):
    bl_size = lax.axis_size("bl")
    bl_index = lax.axis_index("bl")
    inputs_dev = samples.shape[0]
    spec_dev = samples.shape[1] // FRAME
    table = filter_table()
    frames = samples.reshape(inputs_dev, spec_dev, FRAME)
    last_frames = frames[:, spec_dev - (TAPS - 1) :, :]
    earlier = from_behind(last_frames, "bl", 1)
    earlier = jnp.where(bl_index == 0, history.reshape(inputs_dev, TAPS - 1, FRAME), earlier)
    extended = jnp.concatenate([earlier, frames], axis=1)
    accum = jnp.zeros((2 * CH, inputs_dev, spec_dev), jnp.float32)
    for tap_index in range(TAPS):
        accum = accum + jnp.einsum(
            "psn,nk->kps",
            extended[:, tap_index : tap_index + spec_dev],
            table[tap_index],
            preferred_element_type=jnp.float32,
        )
    spectra = accum.astype(jnp.bfloat16).reshape(2, CH, inputs_dev, spec_dev)
    turned = lax.all_to_all(spectra, "ct", split_axis=1, concat_axis=2, tiled=True)
    channels = turned.shape[1]
    inputs = turned.shape[2]
    blocks = inputs // BLOCK
    cell_count = CELL_DEV * bl_size
    weights = tile_weight * (1.0 / math.sqrt(SPECTRA))
    rows_each = blocks // bl_size
    shard_part = lax.all_gather(turned, "bl", axis=3, tiled=True)
    row_part = lax.dynamic_slice_in_dim(
        shard_part, bl_index * rows_each * BLOCK, rows_each * BLOCK, 2
    )
    products = jnp.einsum(
        "acps,bcqs->cabpq", row_part, shard_part, preferred_element_type=jnp.float32
    )
    visibility = jnp.stack(
        [products[:, 0, 0] + products[:, 1, 1], products[:, 1, 0] - products[:, 0, 1]], axis=1
    )
    visibility = visibility.reshape(channels, 2, rows_each, BLOCK, blocks, BLOCK)
    row_index = bl_index * rows_each + jnp.arange(rows_each, dtype=jnp.int32)
    col_index = jnp.arange(blocks, dtype=jnp.int32)
    is_valid = col_index[None, :] >= row_index[:, None]
    tri_index = (
        row_index[:, None] * blocks
        - row_index[:, None] * (row_index[:, None] - 1) // 2
        + col_index[None, :]
        - row_index[:, None]
    )
    tri_index = jnp.where(is_valid, tri_index, 0).reshape(-1)
    selector = cell_selector(
        tile_cell, weights, tri_index, is_valid.reshape(-1).astype(jnp.float32), cell_count
    )
    selector = selector.reshape(cell_count, channels, rows_each, blocks)
    cell_term = jnp.einsum(
        "ecmj,cxmpjq->ecxpq", selector, visibility, precision=lax.Precision.HIGHEST
    )
    return lax.psum_scatter(cell_term, "bl", scatter_dimension=0, tiled=True)


def solution(mesh):
    def whole(samples, history, tile_cell, tile_weight):
        shards = fast_shards if fits(mesh, samples) else general_shards
        return jax.shard_map(
            shards,
            mesh=mesh,
            in_specs=(P("ct", "bl"), P("ct", None), P("ct", None), P("ct", None)),
            out_specs=P("bl", "ct", None, None, None),
            check_vma=False,
        )(samples, history, tile_cell, tile_weight)

    return whole
```

```python
import math

import jax
import jax.numpy as jnp
import numpy as np
from jax import lax
from jax.experimental import pallas as pl
from jax.experimental.pallas import tpu as pltpu
from jax.sharding import PartitionSpec as P

CH = 256
BLOCK = 128
TAPS = 4
SPECTRA = 128
CELL_DEV = 2
FRAME = 512
LANES = 128
SUBLANES = 8
HALO = TAPS - 1
STEP = 8
PIECE = 2


def table_rows():
    span = TAPS * FRAME
    sample_pos = np.arange(span, dtype=np.float64) + 0.5
    window = np.sinc(sample_pos / FRAME - TAPS / 2.0) * (
        0.5 - 0.5 * np.cos(2.0 * math.pi * sample_pos / span)
    )
    phase = np.arange(CH, dtype=np.int64)[:, None] * np.arange(FRAME, dtype=np.int64)[None, :] % FRAME
    angle = phase * (2.0 * math.pi / FRAME)
    basis = np.concatenate([np.cos(angle), -np.sin(angle)], axis=0)
    table = basis[:, None, :] * window.reshape(1, TAPS, FRAME) * (2.0 / math.sqrt(FRAME))
    return table.reshape(2 * CH, span).astype(np.float32).astype(jnp.bfloat16)


def chunk_table(groups, first, count):
    rows = table_rows().reshape(2, groups, CH // groups, TAPS * FRAME)
    rows = rows[:, :, first : first + count].transpose(1, 2, 0, 3)
    return np.ascontiguousarray(rows).reshape(2 * groups * count, TAPS * FRAME)


VMEM = pl.BlockSpec(memory_space=pltpu.VMEM)
SMEM = pl.BlockSpec(memory_space=pltpu.SMEM)
FAR = pl.BlockSpec(memory_space=pltpu.HBM)
LIMIT = pltpu.CompilerParams(vmem_limit_bytes=20 << 20)


def near(value):
    return pltpu.with_memory_space_constraint(value, pltpu.VMEM)


def far(value):
    return pltpu.with_memory_space_constraint(value, pltpu.HBM)


def spectra_of(extended, table, groups):
    window = jnp.concatenate(
        [extended[:, s * FRAME : (s + TAPS) * FRAME] for s in range(STEP)], axis=0
    )
    accum = lax.dot_general(
        table, window, (((1,), (1,)), ((), ())), preferred_element_type=jnp.float32
    )
    pieces = [
        accum[:, at : at + LANES].reshape(groups, -1, LANES)
        for at in range(0, accum.shape[1], LANES)
    ]
    return jnp.concatenate(pieces, axis=1).astype(jnp.bfloat16)


def send_rows(samples, table, groups):
    inputs, length = samples.shape
    return table.shape[0] // groups * (STEP * inputs // LANES), length // FRAME // STEP


def later_steps(src, tab, out, rows, steps, groups, arrived=None):
    def later(step, carry):
        if arrived is not None:
            arrived(step)
        start = pl.multiple_of((step * STEP - HALO) * FRAME, FRAME)
        extended = src[:, pl.ds(start, (STEP + HALO) * FRAME)]
        at = pl.multiple_of(step * rows, rows)
        out[:, pl.ds(at, rows), :] = spectra_of(extended, tab[...], groups)
        return carry

    lax.fori_loop(1, steps, later, 0)


def channelize_early(samples, history, table, groups):
    rows, steps = send_rows(samples, table, groups)

    def body(far_src, far_history, far_tab, out, src, before, tab, sems, extra_sems):
        def bring(step):
            at = pl.multiple_of(step * STEP * FRAME, STEP * FRAME)
            return pltpu.make_async_copy(
                far_src.at[:, pl.ds(at, STEP * FRAME)],
                src.at[:, pl.ds(at, STEP * FRAME)],
                sems.at[step],
            )

        bring_table = pltpu.make_async_copy(far_tab, tab, extra_sems.at[0])
        bring_history = pltpu.make_async_copy(far_history, before, extra_sems.at[1])
        bring_table.start()
        for step in range(steps):
            bring(step).start()
        bring_history.start()
        bring(0).wait()
        bring_table.wait()
        later_steps(src, tab, out, rows, steps, groups, lambda step: bring(step).wait())
        bring_history.wait()

    return pl.pallas_call(
        body,
        in_specs=[FAR, FAR, FAR],
        out_specs=(VMEM,) * 4,
        out_shape=(
            pltpu.VMEM((groups, steps * rows, LANES), jnp.bfloat16),
            pltpu.VMEM(samples.shape, samples.dtype),
            pltpu.VMEM(history.shape, history.dtype),
            pltpu.VMEM(table.shape, table.dtype),
        ),
        scratch_shapes=[pltpu.SemaphoreType.DMA((steps,)), pltpu.SemaphoreType.DMA((2,))],
        compiler_params=LIMIT,
        name="channelize_early",
    )(far(samples), far(history), far(table))


def channelize(samples, table, index, history, behind, so_far, groups):
    rows, steps = send_rows(samples, table, groups)

    def body(index_ref, src, tab, history_ref, behind_ref, *rest):
        def first_step():
            before = jnp.where(index_ref[0] == 0, history_ref[...], behind_ref[...])
            extended = jnp.concatenate([before, src[:, : STEP * FRAME]], axis=1)
            return spectra_of(extended, tab[...], groups)

        if so_far is None:
            out = rest[0]
            out[:, :rows, :] = first_step()
            later_steps(src, tab, out, rows, steps, groups)
            return
        others, out, head, sems = rest
        send_others = pltpu.make_async_copy(
            others.at[:, pl.ds(rows, (steps - 1) * rows), :],
            out.at[:, pl.ds(rows, (steps - 1) * rows), :],
            sems.at[0],
        )
        send_head = pltpu.make_async_copy(head, out.at[:, pl.ds(0, rows), :], sems.at[1])
        send_others.start()
        head[...] = first_step()
        send_head.start()
        send_others.wait()
        send_head.wait()

    args = [near(samples), near(table), near(history), near(behind)]
    shape = (groups, steps * rows, LANES)
    if so_far is None:
        out_spec, out_shape, scratch = VMEM, pltpu.VMEM(shape, jnp.bfloat16), []
    else:
        args.append(near(so_far))
        out_spec, out_shape = FAR, pltpu.HBM(shape, jnp.bfloat16)
        scratch = [pltpu.VMEM((groups, rows, LANES), jnp.bfloat16), pltpu.SemaphoreType.DMA((2,))]
    return pl.pallas_call(
        body,
        in_specs=[SMEM] + [VMEM] * len(args),
        out_specs=out_spec,
        out_shape=out_shape,
        scratch_shapes=scratch,
        compiler_params=LIMIT,
        name="channelize",
    )(index, *args)


def lane_exchange(tiles, width):
    count = len(tiles)
    lane = lax.broadcasted_iota(jnp.int32, tiles[0].shape, 1)
    size = count // 2
    while size:
        span = size * width
        upper = (lane // span) % 2 == 1
        done = list(tiles)
        for a in range(count):
            if a & size:
                continue
            low, high = tiles[a], tiles[a | size]
            done[a] = jnp.where(upper, pltpu.roll(high, span, 1), low)
            done[a | size] = jnp.where(upper, high, pltpu.roll(low, LANES - span, 1))
        tiles = done
        size //= 2
    return tiles


def arrange(turned, inputs_dev):
    ct_size, bl_size, rows, _ = turned.shape
    share = BLOCK // inputs_dev
    blocks = ct_size // share
    pitch = SPECTRA + 1
    per_bl = rows // SUBLANES

    def body(src, columns):
        def relay(step, carry):
            top = pl.multiple_of(step * 2 * SUBLANES, 2 * SUBLANES)
            for b in range(bl_size):
                for block in range(blocks):
                    loaded = [
                        src[block * share + a, b, pl.ds(top, 2 * SUBLANES), :].astype(jnp.float32)
                        for a in range(share)
                    ]
                    for half in range(2):
                        tiles = [t[half * SUBLANES : (half + 1) * SUBLANES] for t in loaded]
                        for s, tile in enumerate(lane_exchange(tiles, inputs_dev)):
                            row = (b * per_bl + step * 2 + half) * share + s
                            columns[block, pl.ds(row, SUBLANES, stride=pitch), :] = tile
            return carry

        lax.fori_loop(0, rows // (2 * SUBLANES), relay, 0)

    return pl.pallas_call(
        body,
        in_specs=[VMEM],
        out_specs=VMEM,
        out_shape=pltpu.VMEM((blocks, SUBLANES * pitch, LANES), jnp.float32),
        compiler_params=LIMIT,
        name="arrange",
    )(near(turned))


def correlate(columns, index, tile_cell, tile_weight, first, skip, channels, bl_size):
    blocks, height, _ = columns.shape
    pitch = height // SUBLANES
    cells = CELL_DEV * bl_size
    group = tile_cell.shape[0] // bl_size

    def body(index_ref, cell_ref, weight_ref, src, own, away, sums):
        mine = index_ref[0]

        def one(local, carry):
            channel = mine * group + first + skip + local
            right = []
            left = []
            for block in range(blocks):
                parts = [
                    src[block, pl.ds((2 * (skip + local) + part) * pitch, SPECTRA), :]
                    for part in range(2)
                ]
                right.append(jnp.concatenate(parts, axis=0).astype(jnp.bfloat16))
                real, imag = [p.T.astype(jnp.bfloat16) for p in parts]
                left.append(
                    jnp.concatenate(
                        [
                            jnp.concatenate([real, imag], axis=1),
                            jnp.concatenate([imag, -real], axis=1),
                        ],
                        axis=0,
                    )
                )
            sums[...] = jnp.zeros_like(sums)
            tile = 0
            for row in range(blocks):
                col = row
                while col < blocks:
                    wide = 1 if (blocks - col) % 2 else 2
                    product = jnp.dot(
                        left[row],
                        jnp.concatenate(right[col : col + wide], axis=1),
                        preferred_element_type=jnp.float32,
                    )
                    for at in range(wide):
                        cell = cell_ref[channel, tile]
                        weight = weight_ref[channel, tile] * (1.0 / math.sqrt(SPECTRA))
                        part = product[:, at * BLOCK : (at + 1) * BLOCK] * weight
                        sums[cell] += part.reshape(2, BLOCK, BLOCK)
                        tile += 1
                    col += wide
            for e in range(CELL_DEV):
                own[local, e] = sums[mine * CELL_DEV + e]
            for step in range(1, bl_size):
                to = lax.rem(mine + step, bl_size)
                for e in range(CELL_DEV):
                    away[step - 1, local, e] = sums[to * CELL_DEV + e].astype(jnp.bfloat16)
            return carry

        lax.fori_loop(0, channels, one, 0)

    flops = channels * blocks * (blocks + 1) // 2 * 4 * 2 * BLOCK * BLOCK * SPECTRA
    return pl.pallas_call(
        body,
        in_specs=[SMEM, SMEM, SMEM, VMEM],
        out_specs=(VMEM, VMEM),
        scratch_shapes=[pltpu.VMEM((cells, 2, BLOCK, BLOCK), jnp.float32)],
        out_shape=(
            pltpu.VMEM((channels, CELL_DEV, 2, BLOCK, BLOCK), jnp.float32),
            pltpu.VMEM((bl_size - 1, channels, CELL_DEV, 2, BLOCK, BLOCK), jnp.bfloat16),
        ),
        compiler_params=LIMIT,
        cost_estimate=pl.CostEstimate(flops=flops, transcendentals=0, bytes_accessed=0),
        name="correlate",
    )(index, tile_cell, tile_weight, near(columns))


def store(grid_so_far, received, owned, index, first, own_channels, bl_size):
    steps, channels = received.shape[:2]
    group = own_channels // bl_size
    fresh = grid_so_far is None

    def body(index_ref, src, *rest):
        out, wide, sems, own_sems = rest[-4:]
        mine = index_ref[0]
        copies = []
        for number, (at, sums) in enumerate(owned):
            for local in range(sums.shape[0]):
                copies.append(
                    pltpu.make_async_copy(
                        rest[number].at[local],
                        out.at[:, mine * group + at + local],
                        own_sems.at[number, local],
                    )
                )
                copies[-1].start()
        for step in range(steps):
            origin = lax.rem(mine + bl_size - 1 - step, bl_size)
            for local in range(channels):
                wide[step, local] = src[step, local].astype(jnp.float32)
                copies.append(
                    pltpu.make_async_copy(
                        wide.at[step, local],
                        out.at[:, origin * group + first + local],
                        sems.at[step, local],
                    )
                )
                copies[-1].start()
        for copy in copies:
            copy.wait()

    most = max([sums.shape[0] for _, sums in owned], default=1)
    args = [near(received)] + [near(sums) for _, sums in owned]
    in_specs = [SMEM] + [VMEM] * len(args)
    aliases = {}
    if not fresh:
        aliases = {len(in_specs): 0}
        in_specs.append(FAR)
        args.append(grid_so_far)
    return pl.pallas_call(
        body,
        in_specs=in_specs,
        out_specs=FAR,
        scratch_shapes=[
            pltpu.VMEM(received.shape, jnp.float32),
            pltpu.SemaphoreType.DMA((steps, channels)),
            pltpu.SemaphoreType.DMA((max(len(owned), 1), most)),
        ],
        out_shape=pltpu.HBM((CELL_DEV, own_channels, 2, BLOCK, BLOCK), jnp.float32),
        input_output_aliases=aliases,
        compiler_params=LIMIT,
        name="store",
    )(index, *args)


def fast_shards(samples, history, tile_cell, tile_weight):
    ct_size = lax.axis_size("ct")
    bl_size = lax.axis_size("bl")
    index = lax.axis_index("bl").reshape(1).astype(jnp.int32)
    inputs_dev = samples.shape[0]
    spec_dev = samples.shape[1] // FRAME
    groups = ct_size * bl_size
    count = SUBLANES // 2
    chunks = range(0, CH // groups, count)

    behind = from_behind(samples[:, (spec_dev - HALO) * FRAME :], "bl", 1)
    received = []
    for number, first in enumerate(chunks):
        table = jnp.asarray(chunk_table(groups, first, count))
        if number == 0:
            early, samples, history, table = channelize_early(samples, history, table, groups)
            spectra = channelize(samples, table, index, history, behind, early, groups)
        else:
            spectra = channelize(samples, table, index, history, behind, None, groups)
        turned = lax.all_to_all(spectra, ("ct", "bl"), 0, 0, tiled=True)
        received.append(turned.reshape(ct_size, bl_size, -1, LANES))
    pieces = []
    for first, turned in zip(chunks, received):
        columns = arrange(turned, inputs_dev)
        piece = PIECE if first == chunks[-1] else count
        for skip in range(0, count, piece):
            own, away = correlate(
                columns, index, tile_cell, tile_weight, first, skip, piece, bl_size
            )
            back = []
            for step in range(1, bl_size):
                pairs = [(i, (i + step) % bl_size) for i in range(bl_size)]
                back.append(lax.ppermute(away[step - 1], "bl", pairs))
            pieces.append((first + skip, own, jnp.stack(back)))
    grid = None
    own_channels = tile_cell.shape[0]
    for number, (first, own, back) in enumerate(pieces):
        owned = [(first, own)]
        if number == len(pieces) - 2:
            owned.append((pieces[-1][0], pieces[-1][1]))
        if number == len(pieces) - 1:
            owned = []
        grid = store(grid, back, owned, index, first, own_channels, bl_size)
    return grid


def fits(mesh, samples):
    ct_size, bl_size = mesh.shape["ct"], mesh.shape["bl"]
    inputs = samples.shape[0]
    spec_dev = samples.shape[1] // FRAME // bl_size
    inputs_dev = inputs // ct_size
    groups = ct_size * bl_size
    return (
        bl_size > 1
        and inputs_dev % 16 == 0
        and LANES % inputs_dev == 0
        and STEP * inputs_dev % LANES == 0
        and spec_dev % STEP == 0
        and spec_dev > STEP
        and inputs % BLOCK == 0
        and CH % groups == 0
        and CH // groups % (SUBLANES // 2) == 0
    )


def from_behind(value, axis, by):
    size = lax.axis_size(axis)
    pairs = [(i, i + by) for i in range(size) if 0 <= i + by < size]
    return lax.ppermute(value, axis, pairs)


def filter_table():
    span = TAPS * FRAME
    sample_pos = jnp.arange(span, dtype=jnp.float32) + 0.5
    window = jnp.sinc(sample_pos / FRAME - TAPS / 2.0) * (
        0.5 - 0.5 * jnp.cos(2.0 * math.pi * sample_pos / span)
    )
    phase_int = (
        jnp.arange(FRAME, dtype=jnp.int32)[:, None]
        * jnp.arange(CH, dtype=jnp.int32)[None, :]
        % FRAME
    )
    angle = phase_int.astype(jnp.float32) * (2.0 * math.pi / FRAME)
    basis = jnp.concatenate([jnp.cos(angle), -jnp.sin(angle)], axis=1)
    table = window.reshape(TAPS, FRAME)[:, :, None] * basis[None] * (2.0 / math.sqrt(FRAME))
    return table.astype(jnp.bfloat16)


def cell_selector(tile_cell, weights, tri_index, is_valid, cell_count):
    picked = jnp.take(tile_cell, tri_index, axis=1)
    picked_weight = jnp.take(weights, tri_index, axis=1) * is_valid
    cell_ids = lax.broadcasted_iota(jnp.int32, (cell_count, 1, 1), 0)
    return (picked[None] == cell_ids).astype(jnp.float32) * picked_weight[None]


def general_shards(samples, history, tile_cell, tile_weight):
    bl_size = lax.axis_size("bl")
    bl_index = lax.axis_index("bl")
    inputs_dev = samples.shape[0]
    spec_dev = samples.shape[1] // FRAME
    table = filter_table()
    frames = samples.reshape(inputs_dev, spec_dev, FRAME)
    last_frames = frames[:, spec_dev - (TAPS - 1) :, :]
    earlier = from_behind(last_frames, "bl", 1)
    earlier = jnp.where(bl_index == 0, history.reshape(inputs_dev, TAPS - 1, FRAME), earlier)
    extended = jnp.concatenate([earlier, frames], axis=1)
    accum = jnp.zeros((2 * CH, inputs_dev, spec_dev), jnp.float32)
    for tap_index in range(TAPS):
        accum = accum + jnp.einsum(
            "psn,nk->kps",
            extended[:, tap_index : tap_index + spec_dev],
            table[tap_index],
            preferred_element_type=jnp.float32,
        )
    spectra = accum.astype(jnp.bfloat16).reshape(2, CH, inputs_dev, spec_dev)
    turned = lax.all_to_all(spectra, "ct", split_axis=1, concat_axis=2, tiled=True)
    channels = turned.shape[1]
    inputs = turned.shape[2]
    blocks = inputs // BLOCK
    cell_count = CELL_DEV * bl_size
    weights = tile_weight * (1.0 / math.sqrt(SPECTRA))
    rows_each = blocks // bl_size
    shard_part = lax.all_gather(turned, "bl", axis=3, tiled=True)
    row_part = lax.dynamic_slice_in_dim(
        shard_part, bl_index * rows_each * BLOCK, rows_each * BLOCK, 2
    )
    products = jnp.einsum(
        "acps,bcqs->cabpq", row_part, shard_part, preferred_element_type=jnp.float32
    )
    visibility = jnp.stack(
        [products[:, 0, 0] + products[:, 1, 1], products[:, 1, 0] - products[:, 0, 1]], axis=1
    )
    visibility = visibility.reshape(channels, 2, rows_each, BLOCK, blocks, BLOCK)
    row_index = bl_index * rows_each + jnp.arange(rows_each, dtype=jnp.int32)
    col_index = jnp.arange(blocks, dtype=jnp.int32)
    is_valid = col_index[None, :] >= row_index[:, None]
    tri_index = (
        row_index[:, None] * blocks
        - row_index[:, None] * (row_index[:, None] - 1) // 2
        + col_index[None, :]
        - row_index[:, None]
    )
    tri_index = jnp.where(is_valid, tri_index, 0).reshape(-1)
    selector = cell_selector(
        tile_cell, weights, tri_index, is_valid.reshape(-1).astype(jnp.float32), cell_count
    )
    selector = selector.reshape(cell_count, channels, rows_each, blocks)
    cell_term = jnp.einsum(
        "ecmj,cxmpjq->ecxpq", selector, visibility, precision=lax.Precision.HIGHEST
    )
    return lax.psum_scatter(cell_term, "bl", scatter_dimension=0, tiled=True)


def solution(mesh):
    def whole(samples, history, tile_cell, tile_weight):
        shards = fast_shards if fits(mesh, samples) else general_shards
        return jax.shard_map(
            shards,
            mesh=mesh,
            in_specs=(P("ct", "bl"), P("ct", None), P("ct", None), P("ct", None)),
            out_specs=P("bl", "ct", None, None, None),
            check_vma=False,
        )(samples, history, tile_cell, tile_weight)

    return whole
```
